32 devices in a mesh: groups: 2 (over y), row: 16 (over z, x, core).
Axes of the slice: x: 2, y: 2, z: 4, core: 2. Of those that a mesh axis runs over, the one named last changes fastest.
Arguments:
- inputs: bfloat16 [32, 8192], P(('groups', 'row')), parts along dimension 0, may hold values from -6 to 6
- out_grad: bfloat16 [32, 8192], P(('groups', 'row')), parts along dimension 0, may hold values from -6 to 6
- gate_weight: bfloat16 [8192, 16384], P(None, 'row'), may hold values from -0.125 to 0.125
- up_weight: bfloat16 [8192, 16384], P(None, 'row'), may hold values from -0.09375 to 0.09375
- down_weight: bfloat16 [16384, 8192], P('row'), may hold values from -0.09375 to 0.09375
- block_mask: int32 [3, 128, 64], P(None, 'row'), may hold values from 0 to 1, as said below
Outputs:
- outputs: bfloat16 [32, 8192], P(('groups', 'row')), parts along dimension 0
- in_grad: bfloat16 [32, 8192], P(('groups', 'row')), parts along dimension 0
- gate_grad: bfloat16 [16384, 16384], P('groups', 'row'), parts along dimension 0
- up_grad: bfloat16 [16384, 16384], P('groups', 'row'), parts along dimension 0
- down_grad: bfloat16 [32768, 8192], P(('groups', 'row')), parts along dimension 0
The draws below stay inside these ranges and needn't reach their ends.
There are 2 independent parts, one for each index of `groups`. The reference program is written for one: setup_inputs(seed, part) draws one part's arguments, and reference() takes and returns one part's arrays. A program takes and returns all parts, laid end to end along the dimension named above; an argument that names none is the same for every part. Nothing has to cross between parts.
Inputs may be any that keep to these rules, and one draw needn't show every extreme that they name: `block_mask`: each entry is 0 or 1. The share of kept blocks differs from hidden block to hidden block, about a quarter to three quarters.
All inputs are finite; a program needn't handle non-finite values.
Results may differ from the reference program's by a relative error of at most 0.005.
Values may be sent and summed in bfloat16 or wider, within the bound.
A program may use at most 256 MiB of HBM per device.

```python
import jax
import jax.numpy as jnp

D = 8192
FF = 16384
BLOCK = 128
TOKENS = 16


def draw_block_mask(key, part):
    level_key = jax.random.fold_in(key, 11)
    coin_key = jax.random.fold_in(key, 23)
    level = jax.random.randint(level_key, (3, FF // BLOCK, 1), 1, 4)
    coin = jax.random.randint(coin_key, (3, FF // BLOCK, D // BLOCK), 0, 4)
    return (coin < level).astype(jnp.int32)


def strengthened(array, stream_key, source, target, blocks, factor):
    owner, partner = [(jnp.arange(array.shape[dim]) // (array.shape[dim] // blocks)).reshape([-1 if axis == dim else 1 for axis in range(array.ndim)]) for dim in (source, target)]
    chosen = jax.random.permutation(stream_key, blocks)[partner]
    strong = (owner == chosen) | (owner == (partner + blocks // 2) % blocks)
    return jnp.where(strong, factor * array, array)


def levels(stream_key, extent, cuts, smallest, high):
    def one(axis_at, shards_of):
        heights = jax.random.uniform(jax.random.fold_in(jax.random.fold_in(stream_key, 6), axis_at), (shards_of,), jnp.float32, smallest / len(cuts), high / len(cuts))
        return jnp.repeat(jnp.exp(heights), extent[axis_at] // shards_of).reshape((-1,) + (1,) * (len(extent) - axis_at - 1))

    factor_of = one(*cuts[0])
    for cut in cuts[1:]:
        factor_of = factor_of * one(*cut)
    return factor_of


def noise(key, extent, deviation, bound, shards=(), held_as=jnp.bfloat16):
    array = deviation * jax.random.normal(key, extent, jnp.float32)
    if shards:
        array = array * levels(key, extent, shards, -0.22, 0.18)
    return jnp.clip(array, -bound, bound).astype(held_as)


def noise_with(stream_key, dims, scale, limit, shards, heavy, dtype=jnp.bfloat16):
    array = scale * jax.random.normal(stream_key, dims, jnp.float32)
    if shards:
        array = array * levels(stream_key, dims, shards, -0.22, 0.18)
    return jnp.clip(strengthened(array, jax.random.fold_in(stream_key, 3), *heavy), -limit, limit).astype(dtype)


def setup_inputs(seed: int = 0, part: int = 0) -> dict:
    seeds = jax.random.split(jax.random.key(seed), 7)
    part_keys = jax.random.split(jax.random.fold_in(seeds[6], part), 7)
    inputs = noise(part_keys[0], (TOKENS, D), 1.0, 6.0, ((0, 16),))
    out_grad = noise(part_keys[1], (TOKENS, D), 1.0, 6.0, ((0, 16),))
    gate_weight = noise_with(seeds[2], (D, FF), (D // 2) ** -0.5, 0.125, ((1, 16),), (1, 0, 16, 2.0))
    up_weight = noise(seeds[3], (D, FF), (D // 2) ** -0.5, 0.09375, ((1, 16),))
    down_weight = noise_with(seeds[4], (FF, D), (FF // 2) ** -0.5, 0.09375, ((0, 16),), (0, 1, 16, 2.0))
    block_mask = draw_block_mask(jax.random.fold_in(seeds[6], 71), part)
    return {"inputs": inputs, "out_grad": out_grad, "gate_weight": gate_weight, "up_weight": up_weight, "down_weight": down_weight, "block_mask": block_mask}


def expand(flags):
    fb, db = flags.shape
    full = jnp.broadcast_to(flags[:, None, :, None], (fb, BLOCK, db, BLOCK))
    return full.reshape(fb * BLOCK, db * BLOCK).astype(jnp.bfloat16)


def reference(inputs, out_grad, gate_weight, up_weight, down_weight, block_mask):
    mask_gate = expand(block_mask[0]).T
    mask_up = expand(block_mask[1]).T
    mask_down = expand(block_mask[2])
    gate_eff = gate_weight * mask_gate
    up_eff = up_weight * mask_up
    down_eff = down_weight * mask_down
    gate = jnp.dot(inputs, gate_eff, preferred_element_type=jnp.float32)
    up = jnp.dot(inputs, up_eff, preferred_element_type=jnp.float32)
    sig = jax.nn.sigmoid(gate)
    hidden = (gate * sig * up).astype(jnp.bfloat16)
    outputs = jnp.dot(hidden, down_eff, preferred_element_type=jnp.float32).astype(jnp.bfloat16)
    hidden_grad = jnp.dot(out_grad, down_eff.T, preferred_element_type=jnp.float32)
    down_grad = (jnp.dot(hidden.T, out_grad, preferred_element_type=jnp.float32) * mask_down.astype(jnp.float32)).astype(jnp.bfloat16)
    gate_delta = (hidden_grad * up * sig * (1.0 + gate * (1.0 - sig))).astype(jnp.bfloat16)
    up_delta = (hidden_grad * gate * sig).astype(jnp.bfloat16)
    gate_grad = (jnp.dot(inputs.T, gate_delta, preferred_element_type=jnp.float32) * mask_gate.astype(jnp.float32)).astype(jnp.bfloat16)
    up_grad = (jnp.dot(inputs.T, up_delta, preferred_element_type=jnp.float32) * mask_up.astype(jnp.float32)).astype(jnp.bfloat16)
    in_grad = jnp.dot(gate_delta, gate_eff.T, preferred_element_type=jnp.float32) + jnp.dot(up_delta, up_eff.T, preferred_element_type=jnp.float32)
    return outputs, in_grad.astype(jnp.bfloat16), gate_grad, up_grad, down_grad
```

```python
import functools

import jax
import jax.numpy as jnp
from jax import lax
from jax.experimental import pallas as pl
from jax.experimental.pallas import tpu as pltpu
from jax.sharding import PartitionSpec as P

BLOCK = 128
SUB = 16
F32, BF16 = jnp.float32, jnp.bfloat16
VM = pltpu.VMEM
MIB = 1 << 20


def dot(a, b, ca=1, cb=0):
    return lax.dot_general(a, b, (((ca,), (cb,)), ((), ())), preferred_element_type=F32)


def spread(rows, cols):
    at = lax.broadcasted_iota(jnp.int32, (rows, cols), 1) // BLOCK
    return (at == lax.broadcasted_iota(jnp.int32, (rows, cols), 0)).astype(BF16)


def diagonal(v, tokens, nb):
    return jnp.concatenate(
        [v[b * tokens:(b + 1) * tokens, b * BLOCK:(b + 1) * BLOCK] for b in range(nb)], axis=1
    )


def layer(n, fc, mine_ref, mask_ref, wg_hbm, wu_hbm, wd_hbm,
          out_ref, hid_ref, gd_ref, ud_ref, x_ref, o_ref, md_ref, mfg_ref, mfu_ref,
          wg, wu, wd, meg, meu, mfd, xm, yacc, iacc, got, part, from_core, chip_sum, from_chips,
          wsem, dsem, gsend, grecv, fsend, csem, rsend, rrecv):
    d = x_ref.shape[1]
    f = hid_ref.shape[1]
    nch = f // fc
    nb = fc // BLOCK
    fb = f // BLOCK
    db = d // BLOCK
    chips = n // 2
    lanes = d // SUB
    me = lax.axis_index("row")
    grp = lax.axis_index("groups")
    chip, core = me // 2, lax.rem(me, 2)
    sib = chip * 2 + (1 - core)

    def weight_copies(c):
        cols = pl.ds(pl.multiple_of(c * fc, fc), fc)
        return (
            pltpu.make_async_copy(wg_hbm.at[:, cols], wg.at[c], wsem.at[0, c]),
            pltpu.make_async_copy(wu_hbm.at[:, cols], wu.at[c], wsem.at[1, c]),
            pltpu.make_async_copy(wd_hbm.at[cols, :], wd.at[c], wsem.at[2, c]),
        )

    for c in range(nch):
        for cp in weight_copies(c):
            cp.start()

    barrier = pltpu.get_barrier_semaphore()

    def peer(j):
        return lax.rem(chip + j, chips)

    def signal(j, carry):
        pl.semaphore_signal(barrier, inc=1, device_id=(grp, peer(j) * 2 + core),
                            device_id_type=pl.DeviceIdType.MESH)
        return carry

    lax.fori_loop(1, chips, signal, 0)
    pl.semaphore_signal(barrier, inc=1, device_id=(grp, sib), device_id_type=pl.DeviceIdType.MESH)
    pl.semaphore_wait(barrier, chips)

    def row_to(j):
        q = peer(j)
        return pltpu.make_async_remote_copy(
            src_ref=mine_ref, dst_ref=got.at[me], send_sem=gsend.at[q], recv_sem=grecv.at[me],
            device_id=(grp, q * 2 + core), device_id_type=pl.DeviceIdType.MESH)

    def row_from(j):
        q = peer(j)
        return pltpu.make_async_remote_copy(
            src_ref=mine_ref, dst_ref=got.at[q * 2 + core], send_sem=gsend.at[q],
            recv_sem=grecv.at[q * 2 + core],
            device_id=(grp, q * 2 + core), device_id_type=pl.DeviceIdType.MESH)

    def forward(j):
        q = peer(j)
        return pltpu.make_async_remote_copy(
            src_ref=got.at[q * 2 + core], dst_ref=got.at[q * 2 + core], send_sem=fsend.at[q],
            recv_sem=grecv.at[q * 2 + core],
            device_id=(grp, sib), device_id_type=pl.DeviceIdType.MESH)

    def forwarded(j):
        q = peer(j)
        return pltpu.make_async_remote_copy(
            src_ref=got.at[q * 2 + 1 - core], dst_ref=got.at[q * 2 + 1 - core],
            send_sem=fsend.at[q], recv_sem=grecv.at[q * 2 + 1 - core],
            device_id=(grp, sib), device_id_type=pl.DeviceIdType.MESH)

    own_to_sib = pltpu.make_async_remote_copy(
        src_ref=mine_ref, dst_ref=got.at[me], send_sem=fsend.at[chip], recv_sem=grecv.at[me],
        device_id=(grp, sib), device_id_type=pl.DeviceIdType.MESH)

    def start_row(j, carry):
        row_to(j).start()
        return carry

    lax.fori_loop(1, chips, start_row, 0)
    own_to_sib.start()
    got[me] = mine_ref[...]

    over_d = spread(db, d)
    over_f = spread(fb, f)
    keep = [mask_ref[k].astype(F32).astype(BF16) for k in range(3)]
    meg[...] = dot(keep[0], over_d)
    meu[...] = dot(keep[1], over_d)
    md_ref[...] = dot(keep[2], over_d)
    mfg_ref[...] = dot(keep[0], over_f, 0, 0)
    mfu_ref[...] = dot(keep[1], over_f, 0, 0)
    mfd[...] = dot(keep[2], over_f, 0, 0)
    yacc[...] = jnp.zeros_like(yacc)
    iacc[...] = jnp.zeros_like(iacc)
    side = SUB * SUB
    at_r = lax.broadcasted_iota(jnp.int32, (side, side), 0)
    at_c = lax.broadcasted_iota(jnp.int32, (side, side), 1)
    swap = (at_c == (at_r % SUB) * SUB + at_r // SUB).astype(BF16)

    def pass_on(j, carry):
        row_from(j).wait_recv()
        forward(j).start()
        return carry

    lax.fori_loop(1, chips, pass_on, 0)

    def take(j, carry):
        forwarded(j).wait_recv()
        return carry

    lax.fori_loop(0, chips, take, 0)

    for g in range(n // SUB):
        for k, whole in ((0, x_ref), (1, o_ref)):
            v = got[g * SUB:(g + 1) * SUB, k].reshape(side, lanes)
            v = dot(swap, v).astype(BF16)
            for s in range(SUB):
                whole[g * SUB:(g + 1) * SUB, s * lanes:(s + 1) * lanes] = v[s * SUB:(s + 1) * SUB]

    width = 2 * BLOCK

    def masked_rows(src, mref, c):
        for b in range(nb):
            row = mref[pl.ds(c * nb + b, 1), :].astype(BF16)
            xm[b * n:(b + 1) * n, :] = src[...] * row

    def chunk(c, carry):
        cols = pl.ds(pl.multiple_of(c * fc, fc), fc)
        cg, cu, cd = weight_copies(c)
        masked_rows(x_ref, meg, c)
        cg.wait()
        gate = diagonal(dot(xm[...], wg[c]), n, nb)
        masked_rows(x_ref, meu, c)
        cu.wait()
        up = diagonal(dot(xm[...], wu[c]), n, nb)
        masked_rows(o_ref, md_ref, c)
        cd.wait()
        hg = diagonal(dot(xm[...], wd[c], 1, 1), n, nb)
        sig = jax.nn.sigmoid(gate)
        hid = (gate * sig * up).astype(BF16)
        gd = (hg * up * sig * (1.0 + gate * (1.0 - sig))).astype(BF16)
        ud = (hg * gate * sig).astype(BF16)
        hid_ref[:, cols] = hid
        gd_ref[:, cols] = gd
        ud_ref[:, cols] = ud

        def stacked(v, mref, j):
            return jnp.concatenate(
                [v * mref[pl.ds(2 * j + b, 1), cols].astype(BF16) for b in range(2)], axis=0)

        def feature(j, carry):
            dc = pl.ds(pl.multiple_of(j * width, width), width)
            y = dot(stacked(hid, mfd, j), wd[c, :, dc])
            yacc[:, dc] += diagonal(y, n, 2)
            i = dot(stacked(gd, mfg_ref, j), wg[c, dc, :], 1, 1)
            i += dot(stacked(ud, mfu_ref, j), wu[c, dc, :], 1, 1)
            iacc[:, dc] += diagonal(i, n, 2)
            return carry

        lax.fori_loop(0, d // width, feature, 0, unroll=4)
        return carry

    lax.fori_loop(0, nch, chunk, 0)

    for g in range(n // SUB):
        for k, acc in ((0, yacc), (1, iacc)):
            v = jnp.concatenate(
                [acc[g * SUB:(g + 1) * SUB, s * lanes:(s + 1) * lanes] for s in range(SUB)],
                axis=0).astype(BF16)
            v = dot(swap, v).astype(BF16)
            for t in range(SUB):
                part[t % 2, g * (SUB // 2) + t // 2, k] = v[t * SUB:(t + 1) * SUB]

    swap_cores = pltpu.make_async_remote_copy(
        src_ref=part.at[1 - core], dst_ref=from_core, send_sem=csem.at[0], recv_sem=csem.at[1],
        device_id=(grp, sib), device_id_type=pl.DeviceIdType.MESH)
    swap_cores.start()
    swap_cores.wait()

    def to_chip(j):
        q = peer(j)
        return pltpu.make_async_remote_copy(
            src_ref=chip_sum.at[q], dst_ref=from_chips.at[chip], send_sem=rsend.at[q],
            recv_sem=rrecv.at[chip],
            device_id=(grp, q * 2 + core), device_id_type=pl.DeviceIdType.MESH)

    def from_chip(j):
        q = peer(j)
        return pltpu.make_async_remote_copy(
            src_ref=chip_sum.at[q], dst_ref=from_chips.at[q], send_sem=rsend.at[q],
            recv_sem=rrecv.at[q],
            device_id=(grp, q * 2 + core), device_id_type=pl.DeviceIdType.MESH)

    def send_sum(j, carry):
        q = peer(j)
        chip_sum[q] = (part[core, q].astype(F32) + from_core[q].astype(F32)).astype(BF16)
        to_chip(j).start()
        return carry

    lax.fori_loop(1, chips, send_sum, 0)
    total = part[core, chip].astype(F32) + from_core[chip].astype(F32)

    def add_sum(j, total):
        from_chip(j).wait_recv()
        return total + from_chips[peer(j)].astype(F32)

    total = lax.fori_loop(1, chips, add_sum, total)
    out_ref[...] = total.astype(BF16)

    def drain(j, carry):
        row_to(j).wait_send()
        forward(j).wait_send()
        to_chip(j).wait_send()
        return carry

    lax.fori_loop(1, chips, drain, 0)
    own_to_sib.wait_send()


def grads(x_ref, o_ref, hid_ref, gd_ref, ud_ref, md_ref, mfg_ref, mfu_ref,
          gg_ref, ug_ref, dg_ref):
    i = pl.program_id(0)
    rows = gg_ref.shape[0]
    blocks = rows // BLOCK
    for b in range(blocks):
        at = slice(b * BLOCK, (b + 1) * BLOCK)
        xb = x_ref[:, at]
        row = pl.ds(i * blocks + b, 1)
        gg_ref[at, :] = dot(xb, gd_ref[...] * mfg_ref[row, :].astype(BF16), 0, 0).astype(BF16)
        ug_ref[at, :] = dot(xb, ud_ref[...] * mfu_ref[row, :].astype(BF16), 0, 0).astype(BF16)
    hid = hid_ref[...]
    d = o_ref.shape[1]
    step = min(d, 1024)
    for c in range(d // step):
        at = slice(c * step, (c + 1) * step)
        og = o_ref[:, at] * md_ref[pl.ds(i, 1), at].astype(BF16)
        dg_ref[:, at] = dot(hid, og, 0, 0).astype(BF16)


def per_device(n, inputs, out_grad, gate_weight, up_weight, down_weight, block_mask):
    d, f = gate_weight.shape
    fc = min(f, 2 * BLOCK)
    nch = f // fc
    nb = fc // BLOCK
    fb, db = f // BLOCK, d // BLOCK
    chips = n // 2
    lanes = d // SUB
    mine = jnp.concatenate([inputs, out_grad], axis=0).reshape(2, SUB, lanes)
    vmem = pl.BlockSpec(memory_space=pltpu.VMEM)
    hbm = pl.BlockSpec(memory_space=pl.ANY)
    S = jax.ShapeDtypeStruct
    dma = pltpu.SemaphoreType.DMA
    out, hid, gd, ud, x, o, md, mfg, mfu = pl.pallas_call(
        functools.partial(layer, n, fc),
        out_shape=(S((2, SUB, lanes), BF16), S((n, f), BF16), S((n, f), BF16), S((n, f), BF16),
                   S((n, d), BF16), S((n, d), BF16), S((fb, d), F32), S((db, f), F32),
                   S((db, f), F32)),
        in_specs=[vmem, vmem, hbm, hbm, hbm],
        out_specs=(vmem,) * 9,
        scratch_shapes=[
            VM((nch, d, fc), BF16), VM((nch, d, fc), BF16), VM((nch, fc, d), BF16),
            VM((fb, d), F32), VM((fb, d), F32), VM((db, f), F32), VM((nb * n, d), BF16),
            VM((n, d), F32), VM((n, d), F32),
            VM((n, 2, SUB, lanes), BF16), VM((2, chips, 2, SUB, lanes), BF16),
            VM((chips, 2, SUB, lanes), BF16), VM((chips, 2, SUB, lanes), BF16),
            VM((chips, 2, SUB, lanes), BF16),
            dma((3, nch)), dma((1,)), dma((chips,)), dma((n,)), dma((chips,)), dma((2,)),
            dma((chips,)), dma((chips,)),
        ],
        compiler_params=pltpu.CompilerParams(
            collective_id=0, has_side_effects=True, vmem_limit_bytes=61 * MIB),
        name="layer",
    )(mine, block_mask, gate_weight, up_weight, down_weight)

    rows = d // fb
    full = lambda *shape: pl.BlockSpec(shape, lambda i: (0,) * len(shape))
    gg, ug, dg = pl.pallas_call(
        grads,
        grid=(fb,),
        out_shape=(S((d, f), BF16), S((d, f), BF16), S((f, d), BF16)),
        in_specs=[pl.BlockSpec((n, rows), lambda i: (0, i)), full(n, d),
                  pl.BlockSpec((n, BLOCK), lambda i: (0, i)), full(n, f), full(n, f),
                  full(fb, d), full(db, f), full(db, f)],
        out_specs=(pl.BlockSpec((rows, f), lambda i: (i, 0)),
                   pl.BlockSpec((rows, f), lambda i: (i, 0)),
                   pl.BlockSpec((BLOCK, d), lambda i: (i, 0))),
        compiler_params=pltpu.CompilerParams(vmem_limit_bytes=48 * MIB),
        name="grads",
    )(x, o, hid, gd, ud, md, mfg, mfu)
    out = out.reshape(2, d)
    return out[0:1], out[1:2], gg, ug, dg


def solution(mesh):
    in_specs = (
        P(("groups", "row"), None),
        P(("groups", "row"), None),
        P(None, "row"),
        P(None, "row"),
        P("row", None),
        P(None, "row", None),
    )
    out_specs = (
        P(("groups", "row"), None),
        P(("groups", "row"), None),
        P("groups", "row"),
        P("groups", "row"),
        P(("groups", "row"), None),
    )
    return jax.shard_map(
        functools.partial(per_device, mesh.shape["row"]),
        mesh=mesh, in_specs=in_specs, out_specs=out_specs, check_vma=False,
    )
```

```python
import functools

import jax
import jax.numpy as jnp
from jax import lax
from jax.experimental import pallas as pl
from jax.experimental.pallas import tpu as pltpu
from jax.sharding import PartitionSpec as P

BLOCK = 128
SUB = 16
F32, BF16 = jnp.float32, jnp.bfloat16
VM = pltpu.VMEM
MIB = 1 << 20


def dot(a, b, ca=1, cb=0):
    return lax.dot_general(a, b, (((ca,), (cb,)), ((), ())), preferred_element_type=F32)


def spread(rows, cols):
    at = lax.broadcasted_iota(jnp.int32, (rows, cols), 1) // BLOCK
    return (at == lax.broadcasted_iota(jnp.int32, (rows, cols), 0)).astype(BF16)


def diagonal(v, tokens, nb):
    return jnp.concatenate(
        [v[b * tokens:(b + 1) * tokens, b * BLOCK:(b + 1) * BLOCK] for b in range(nb)], axis=1
    )


def layer(n, fc, mine_ref, mask_ref, wg_hbm, wu_hbm, wd_hbm,
          out_ref, hid_ref, gd_ref, ud_ref, x_ref, o_ref, md_ref, mfg_ref, mfu_ref,
          wg, wu, wd, meg, meu, mfd, xm, yacc, iacc, got, part, from_core, chip_sum, from_chips,
          wsem, dsem, gsend, grecv, fsend, csem, rsend, rrecv):
    d = x_ref.shape[1]
    f = hid_ref.shape[1]
    nch = f // fc
    nb = fc // BLOCK
    fb = f // BLOCK
    db = d // BLOCK
    chips = n // 2
    lanes = d // SUB
    me = lax.axis_index("row")
    grp = lax.axis_index("groups")
    chip, core = me // 2, lax.rem(me, 2)
    sib = chip * 2 + (1 - core)

    def weight_copies(c):
        cols = pl.ds(pl.multiple_of(c * fc, fc), fc)
        return (
            pltpu.make_async_copy(wg_hbm.at[:, cols], wg.at[c], wsem.at[0, c]),
            pltpu.make_async_copy(wu_hbm.at[:, cols], wu.at[c], wsem.at[1, c]),
            pltpu.make_async_copy(wd_hbm.at[cols, :], wd.at[c], wsem.at[2, c]),
        )

    for c in range(nch):
        for cp in weight_copies(c):
            cp.start()

    barrier = pltpu.get_barrier_semaphore()

    def peer(j):
        return lax.rem(chip + j, chips)

    def signal(j, carry):
        pl.semaphore_signal(barrier, inc=1, device_id=(grp, peer(j) * 2 + core),
                            device_id_type=pl.DeviceIdType.MESH)
        return carry

    lax.fori_loop(1, chips, signal, 0)
    pl.semaphore_signal(barrier, inc=1, device_id=(grp, sib), device_id_type=pl.DeviceIdType.MESH)
    pl.semaphore_wait(barrier, chips)

    def row_to(j):
        q = peer(j)
        return pltpu.make_async_remote_copy(
            src_ref=mine_ref, dst_ref=got.at[me], send_sem=gsend.at[q], recv_sem=grecv.at[me],
            device_id=(grp, q * 2 + core), device_id_type=pl.DeviceIdType.MESH)

    def row_from(j):
        q = peer(j)
        return pltpu.make_async_remote_copy(
            src_ref=mine_ref, dst_ref=got.at[q * 2 + core], send_sem=gsend.at[q],
            recv_sem=grecv.at[q * 2 + core],
            device_id=(grp, q * 2 + core), device_id_type=pl.DeviceIdType.MESH)

    def forward(j):
        q = peer(j)
        return pltpu.make_async_remote_copy(
            src_ref=got.at[q * 2 + core], dst_ref=got.at[q * 2 + core], send_sem=fsend.at[q],
            recv_sem=grecv.at[q * 2 + core],
            device_id=(grp, sib), device_id_type=pl.DeviceIdType.MESH)

    def forwarded(j):
        q = peer(j)
        return pltpu.make_async_remote_copy(
            src_ref=got.at[q * 2 + 1 - core], dst_ref=got.at[q * 2 + 1 - core],
            send_sem=fsend.at[q], recv_sem=grecv.at[q * 2 + 1 - core],
            device_id=(grp, sib), device_id_type=pl.DeviceIdType.MESH)

    own_to_sib = pltpu.make_async_remote_copy(
        src_ref=mine_ref, dst_ref=got.at[me], send_sem=fsend.at[chip], recv_sem=grecv.at[me],
        device_id=(grp, sib), device_id_type=pl.DeviceIdType.MESH)

    def start_row(j, carry):
        row_to(j).start()
        return carry

    lax.fori_loop(1, chips, start_row, 0)
    own_to_sib.start()
    got[me] = mine_ref[...]

    over_d = spread(db, d)
    over_f = spread(fb, f)
    keep = [mask_ref[k].astype(F32).astype(BF16) for k in range(3)]
    meg[...] = dot(keep[0], over_d)
    meu[...] = dot(keep[1], over_d)
    md_ref[...] = dot(keep[2], over_d)
    mfg_ref[...] = dot(keep[0], over_f, 0, 0)
    mfu_ref[...] = dot(keep[1], over_f, 0, 0)
    mfd[...] = dot(keep[2], over_f, 0, 0)
    side = SUB * SUB
    at_r = lax.broadcasted_iota(jnp.int32, (side, side), 0)
    at_c = lax.broadcasted_iota(jnp.int32, (side, side), 1)
    swap = (at_c == (at_r % SUB) * SUB + at_r // SUB).astype(BF16)

    def pass_on(j, carry):
        row_from(j).wait_recv()
        forward(j).start()
        return carry

    lax.fori_loop(1, chips, pass_on, 0)

    def take(j, carry):
        forwarded(j).wait_recv()
        return carry

    lax.fori_loop(0, chips, take, 0)

    for g in range(n // SUB):
        for k, whole in ((0, x_ref), (1, o_ref)):
            v = got[g * SUB:(g + 1) * SUB, k].reshape(side, lanes)
            v = dot(swap, v).astype(BF16)
            for s in range(SUB):
                whole[g * SUB:(g + 1) * SUB, s * lanes:(s + 1) * lanes] = v[s * SUB:(s + 1) * SUB]

    width = 2 * BLOCK

    def masked_rows(src, mref, c):
        for b in range(nb):
            row = mref[pl.ds(c * nb + b, 1), :].astype(BF16)
            xm[b * n:(b + 1) * n, :] = src[...] * row

    def chunk(c, carry):
        cols = pl.ds(pl.multiple_of(c * fc, fc), fc)
        cg, cu, cd = weight_copies(c)
        masked_rows(x_ref, meg, c)
        cg.wait()
        gate = diagonal(dot(xm[...], wg[c]), n, nb)
        masked_rows(x_ref, meu, c)
        cu.wait()
        up = diagonal(dot(xm[...], wu[c]), n, nb)
        masked_rows(o_ref, md_ref, c)
        cd.wait()
        hg = diagonal(dot(wd[c], xm[...], 1, 1).T, n, nb)
        sig = jax.nn.sigmoid(gate)
        hid = (gate * sig * up).astype(BF16)
        gd = (hg * up * sig * (1.0 + gate * (1.0 - sig))).astype(BF16)
        ud = (hg * gate * sig).astype(BF16)
        hid_ref[:, cols] = hid
        gd_ref[:, cols] = gd
        ud_ref[:, cols] = ud

        return carry

    lax.fori_loop(0, nch, chunk, 0)

    def stacked(ref, mref, j, c):
        cols = slice(c * fc, (c + 1) * fc)
        return jnp.concatenate(
            [ref[:, cols] * mref[pl.ds(2 * j + b, 1), cols].astype(BF16) for b in range(2)], axis=0)

    def y_feature(j, carry):
        dc = pl.ds(pl.multiple_of(j * width, width), width)
        y = dot(stacked(hid_ref, mfd, j, 0), wd[0, :, dc])
        for c in range(1, nch):
            y += dot(stacked(hid_ref, mfd, j, c), wd[c, :, dc])
        yacc[:, dc] = diagonal(y, n, 2)
        return carry

    def in_feature(j, carry):
        dc = pl.ds(pl.multiple_of(j * width, width), width)
        i = dot(stacked(gd_ref, mfg_ref, j, 0), wg[0, dc, :], 1, 1)
        for c in range(1, nch):
            i += dot(stacked(gd_ref, mfg_ref, j, c), wg[c, dc, :], 1, 1)
        for c in range(nch):
            i += dot(stacked(ud_ref, mfu_ref, j, c), wu[c, dc, :], 1, 1)
        iacc[:, dc] = diagonal(i, n, 2)
        return carry

    def pack(k, acc):
        for g in range(n // SUB):
            v = jnp.concatenate(
                [acc[g * SUB:(g + 1) * SUB, s * lanes:(s + 1) * lanes] for s in range(SUB)],
                axis=0).astype(BF16)
            v = dot(swap, v).astype(BF16)
            for t in range(SUB):
                part[t % 2, k, g * (SUB // 2) + t // 2] = v[t * SUB:(t + 1) * SUB]

    def swap_cores(k):
        return pltpu.make_async_remote_copy(
            src_ref=part.at[1 - core, k], dst_ref=from_core.at[k], send_sem=csem.at[k, 0],
            recv_sem=csem.at[k, 1],
            device_id=(grp, sib), device_id_type=pl.DeviceIdType.MESH)

    def to_chip(k, j):
        q = peer(j)
        return pltpu.make_async_remote_copy(
            src_ref=chip_sum.at[k, q], dst_ref=from_chips.at[k, chip], send_sem=rsend.at[k, q],
            recv_sem=rrecv.at[k, chip],
            device_id=(grp, q * 2 + core), device_id_type=pl.DeviceIdType.MESH)

    def from_chip(k, j):
        q = peer(j)
        return pltpu.make_async_remote_copy(
            src_ref=chip_sum.at[k, q], dst_ref=from_chips.at[k, q], send_sem=rsend.at[k, q],
            recv_sem=rrecv.at[k, q],
            device_id=(grp, q * 2 + core), device_id_type=pl.DeviceIdType.MESH)

    def send_sums(k):
        swap_cores(k).wait()

        def send_sum(j, carry):
            q = peer(j)
            chip_sum[k, q] = (part[core, k, q].astype(F32) + from_core[k, q].astype(F32)).astype(BF16)
            to_chip(k, j).start()
            return carry

        lax.fori_loop(1, chips, send_sum, 0)

    def finish(k):
        def add_sum(j, total):
            from_chip(k, j).wait_recv()
            return total + from_chips[k, peer(j)].astype(F32)

        total = part[core, k, chip].astype(F32) + from_core[k, chip].astype(F32)
        out_ref[k] = lax.fori_loop(1, chips, add_sum, total).astype(BF16)

    tiles = d // width
    lax.fori_loop(0, tiles, y_feature, 0, unroll=4)
    pack(0, yacc)
    swap_cores(0).start()
    lax.fori_loop(0, tiles // 4, in_feature, 0, unroll=2)
    send_sums(0)
    lax.fori_loop(tiles // 4, tiles, in_feature, 0, unroll=2)
    pack(1, iacc)
    swap_cores(1).start()
    send_sums(1)
    finish(0)
    finish(1)

    def drain(j, carry):
        row_to(j).wait_send()
        forward(j).wait_send()
        to_chip(0, j).wait_send()
        to_chip(1, j).wait_send()
        return carry

    lax.fori_loop(1, chips, drain, 0)
    own_to_sib.wait_send()


def grads(x_ref, o_ref, hid_ref, gd_ref, ud_ref, md_ref, mfg_ref, mfu_ref,
          gg_ref, ug_ref, dg_ref):
    i = pl.program_id(0)
    rows = gg_ref.shape[0]
    blocks = rows // BLOCK
    for b in range(blocks):
        at = slice(b * BLOCK, (b + 1) * BLOCK)
        xb = x_ref[:, at]
        row = pl.ds(i * blocks + b, 1)
        gg_ref[at, :] = dot(xb, gd_ref[...] * mfg_ref[row, :].astype(BF16), 0, 0).astype(BF16)
        ug_ref[at, :] = dot(xb, ud_ref[...] * mfu_ref[row, :].astype(BF16), 0, 0).astype(BF16)
    hid = hid_ref[...]
    d = o_ref.shape[1]
    step = min(d, 1024)
    for c in range(d // step):
        at = slice(c * step, (c + 1) * step)
        og = o_ref[:, at] * md_ref[pl.ds(i, 1), at].astype(BF16)
        dg_ref[:, at] = dot(hid, og, 0, 0).astype(BF16)


def per_device(n, inputs, out_grad, gate_weight, up_weight, down_weight, block_mask):
    d, f = gate_weight.shape
    fc = min(f, 2 * BLOCK)
    nch = f // fc
    nb = fc // BLOCK
    fb, db = f // BLOCK, d // BLOCK
    chips = n // 2
    lanes = d // SUB
    mine = jnp.concatenate([inputs, out_grad], axis=0).reshape(2, SUB, lanes)
    vmem = pl.BlockSpec(memory_space=pltpu.VMEM)
    hbm = pl.BlockSpec(memory_space=pl.ANY)
    S = jax.ShapeDtypeStruct
    dma = pltpu.SemaphoreType.DMA
    out, hid, gd, ud, x, o, md, mfg, mfu = pl.pallas_call(
        functools.partial(layer, n, fc),
        out_shape=(S((2, SUB, lanes), BF16), S((n, f), BF16), S((n, f), BF16), S((n, f), BF16),
                   S((n, d), BF16), S((n, d), BF16), S((fb, d), F32), S((db, f), F32),
                   S((db, f), F32)),
        in_specs=[vmem, vmem, hbm, hbm, hbm],
        out_specs=(vmem,) * 9,
        scratch_shapes=[
            VM((nch, d, fc), BF16), VM((nch, d, fc), BF16), VM((nch, fc, d), BF16),
            VM((fb, d), F32), VM((fb, d), F32), VM((db, f), F32), VM((nb * n, d), BF16),
            VM((n, d), F32), VM((n, d), F32),
            VM((n, 2, SUB, lanes), BF16), VM((2, 2, chips, SUB, lanes), BF16),
            VM((2, chips, SUB, lanes), BF16), VM((2, chips, SUB, lanes), BF16),
            VM((2, chips, SUB, lanes), BF16),
            dma((3, nch)), dma((1,)), dma((chips,)), dma((n,)), dma((chips,)), dma((2, 2)),
            dma((2, chips)), dma((2, chips)),
        ],
        compiler_params=pltpu.CompilerParams(
            collective_id=0, has_side_effects=True, vmem_limit_bytes=61 * MIB),
        name="layer",
    )(mine, block_mask, gate_weight, up_weight, down_weight)

    rows = d // fb
    full = lambda *shape: pl.BlockSpec(shape, lambda i: (0,) * len(shape))
    gg, ug, dg = pl.pallas_call(
        grads,
        grid=(fb,),
        out_shape=(S((d, f), BF16), S((d, f), BF16), S((f, d), BF16)),
        in_specs=[pl.BlockSpec((n, rows), lambda i: (0, i)), full(n, d),
                  pl.BlockSpec((n, BLOCK), lambda i: (0, i)), full(n, f), full(n, f),
                  full(fb, d), full(db, f), full(db, f)],
        out_specs=(pl.BlockSpec((rows, f), lambda i: (i, 0)),
                   pl.BlockSpec((rows, f), lambda i: (i, 0)),
                   pl.BlockSpec((BLOCK, d), lambda i: (i, 0))),
        compiler_params=pltpu.CompilerParams(vmem_limit_bytes=61 * MIB),
        name="grads",
    )(x, o, hid, gd, ud, md, mfg, mfu)
    out = out.reshape(2, d)
    return out[0:1], out[1:2], gg, ug, dg


def solution(mesh):
    in_specs = (
        P(("groups", "row"), None),
        P(("groups", "row"), None),
        P(None, "row"),
        P(None, "row"),
        P("row", None),
        P(None, "row", None),
    )
    out_specs = (
        P(("groups", "row"), None),
        P(("groups", "row"), None),
        P("groups", "row"),
        P("groups", "row"),
        P(("groups", "row"), None),
    )
    return jax.shard_map(
        functools.partial(per_device, mesh.shape["row"]),
        mesh=mesh, in_specs=in_specs, out_specs=out_specs, check_vma=False,
    )
```
